128 devices in a mesh: row: 4 (over x), col: 4 (over y), ka: 8 (over z, core).
Axes of the slice: x: 4, y: 4, z: 4, core: 2. Of those that a mesh axis runs over, the one named last changes fastest.
Arguments:
- amplitudes: float32 [5120, 32768], P(('row', 'col', 'ka')), may hold values from -6 to 6
- ladder: float32 [8, 2048, 32768], P(None, 'row', ('col', 'ka')), may hold values from -0.03125 to 0.03125
- pair_energy: float32 [5120], P(('col', 'ka')), may hold values from -3 to -0.5
- vir_energy: float32 [8, 2048], P(None, 'row'), may hold values from 0.5 to 4
- occ_count: int32 [8], replicated, may hold values from 1 to 1024, 5120 in all
- vir_count: int32 [8], replicated, may hold values from 1 to 32768, 163840 in all
Outputs:
- update: float32 [5120, 2048], P(('col', 'ka'), 'row')
The draws below stay inside these ranges and needn't reach their ends.
Inputs may be any that keep to these rules, and one draw needn't show every extreme that they name: `occ_count`: each irrep holds at least one pair; the counts of all 8 irreps sum to 5120, and one irrep holds 1024. `vir_count`: the counts of all 8 irreps sum to 163840, and one irrep fills all 32768 slots.
All inputs are finite; a program needn't handle non-finite values.
Results may differ from the reference program's by a relative error of at most 0.0001.
Values sent between devices are 32-bit elements; how exact they have to be, the bound alone decides.
No kernel may reach another device: no remote copies, remote signals or barrier semaphores. Data moves between devices by JAX's collectives and lax.ppermute only.
A program may use at most 192 MiB of HBM per device.

```python
import math
import jax
import jax.numpy as jnp
import numpy as np
from jax import lax

IRR = 8
CAP = 32768
OCC = 1024
AB = 2048
TOTAL = 5120


def shard_levels(key, extent, shards, least, largest):
    def one(dim, shards_of):
        steps = jax.random.uniform(jax.random.fold_in(jax.random.fold_in(key, 6), dim), (shards_of,), jnp.float32, least / len(shards), largest / len(shards))
        return jnp.repeat(jnp.exp(steps), extent[dim] // shards_of).reshape((-1,) + (1,) * (len(extent) - dim - 1))

    gain = one(*shards[0])
    for cut in shards[1:]:
        gain = gain * one(*cut)
    return gain


def profile(amount, total, reach, lean):
    loads = [(1 << 20) // math.isqrt(rank ** lean) + 1 for rank in range(2, amount + 1)]
    surplus, holding = total - reach - (amount - 1), [1] * (amount - 1)
    while surplus > 0:
        free = [i for i in range(amount - 1) if holding[i] < reach]
        mass, left = sum([loads[i] for i in free]), surplus
        for i in free:
            more = min(reach - holding[i], max(1, left * loads[i] // mass), surplus)
            holding[i] = holding[i] + more
            surplus = surplus - more
    return np.array([reach] + holding)


def uneven_parts(own_key, amount, total, limit, skew):
    if amount == 2:
        one = jax.random.randint(own_key, (), max(1, total - limit), min(limit, total - 1) + 1)
        return jnp.stack([one, total - one])
    tallies = jnp.asarray(profile(amount, total, limit, skew), jnp.int32)
    twos = (amount - 1) // 2
    source_of, receiver = tallies[1:1 + 2 * twos:2], tallies[2:2 + 2 * twos:2]
    slack = jnp.minimum(source_of - 1, limit - receiver)
    moved = jax.random.randint(jax.random.fold_in(own_key, 1), (twos,), 0, 1 << 20) % (slack + 1)
    tallies = tallies.at[1:1 + 2 * twos:2].set(source_of - moved).at[2:2 + 2 * twos:2].set(receiver + moved)
    return tallies[jax.random.permutation(jax.random.fold_in(own_key, 2), amount)]


def noise(own_key, dims, width, bound, cuts=(), held_as=jnp.bfloat16):
    gain = shard_levels(own_key, dims, cuts, -0.22, 0.18) if cuts else 1.0
    array = jax.random.normal(own_key, dims, jnp.float32) * width * gain
    return jnp.minimum(jnp.maximum(array, -bound), bound).astype(held_as)


def setup_inputs(seed: int = 0) -> dict:
    streams_of = jax.random.split(jax.random.key(seed), 7)
    return {
        "amplitudes": noise(streams_of[0], (TOTAL, CAP), 1.0, 6.0, ((0, 128),), jnp.float32),
        "ladder": noise(streams_of[1], (IRR, AB, CAP), CAP ** -0.5, 0.03125, ((1, 4), (2, 32)), jnp.float32),
        "pair_energy": jnp.clip(-3.0 + 2.5 * jax.random.uniform(streams_of[2], (TOTAL,), jnp.float32) ** shard_levels(streams_of[2], (TOTAL,), ((0, 32),), -0.2, 0.2), -3.0, -0.5),
        "vir_energy": jnp.clip(0.5 + 3.5 * jax.random.uniform(streams_of[3], (IRR, AB), jnp.float32) ** shard_levels(streams_of[3], (IRR, AB), ((1, 4),), -0.2, 0.2), 0.5, 4.0),
        "occ_count": uneven_parts(streams_of[4], IRR, 5 * OCC, OCC, 2).astype(jnp.int32),
        "vir_count": uneven_parts(streams_of[5], IRR, 5 * CAP, CAP, 2).astype(jnp.int32),
    }


def reference(amplitudes, ladder, pair_energy, vir_energy, occ_count, vir_count):
    ends = jnp.cumsum(occ_count).astype(jnp.int32)
    starts = (ends - occ_count).astype(jnp.int32)
    positions = jnp.arange(TOTAL, dtype=jnp.int32)
    irrep = jnp.sum((positions[:, None] >= ends[None, :]).astype(jnp.int32), axis=1).astype(jnp.int32)
    cd_mask = (jnp.arange(CAP, dtype=jnp.int32)[None, :] < vir_count[:, None]).astype(jnp.float32)
    ladder_sum = jnp.zeros((TOTAL, AB), jnp.float32)
    for group in range(IRR):
        masked = ladder[group] * cd_mask[group][None, :]
        first = jnp.minimum(starts[group], TOTAL - OCC).astype(jnp.int32)
        window = lax.dynamic_slice_in_dim(amplitudes, first, OCC, 0)
        product = jnp.dot(window, masked.T, precision=lax.Precision.HIGHEST, preferred_element_type=jnp.float32)
        chosen = lax.dynamic_slice_in_dim(irrep, first, OCC, 0) == group
        current = lax.dynamic_slice_in_dim(ladder_sum, first, OCC, 0)
        current = current + jnp.where(chosen[:, None], product, jnp.float32(0.0))
        ladder_sum = lax.dynamic_update_slice_in_dim(ladder_sum, current, first, 0)
    vir_rows = vir_energy[irrep]
    vir_mask = jnp.arange(AB, dtype=jnp.int32)[None, :] < vir_count[irrep][:, None]
    denom = vir_rows - pair_energy[:, None]
    return jnp.where(vir_mask, ladder_sum / denom, jnp.float32(0.0))
```

```python
import jax
import jax.numpy as jnp
from jax import lax
from jax.experimental import pallas as pl
from jax.experimental.pallas import tpu as pltpu
from jax.sharding import PartitionSpec as P

STEP = 8
TILE = 256


def split(value):
    high = value.astype(jnp.bfloat16)
    return high, (value - high.astype(jnp.float32)).astype(jnp.bfloat16)


def split_kernel(count_ref, ladder_ref, high_ref, low_ref):
    group = pl.program_id(0)
    value = ladder_ref[0]
    column = lax.broadcasted_iota(jnp.int32, value.shape, 1)
    value = jnp.where(column < count_ref[group], value, jnp.float32(0.0))
    high, low = split(value)
    high_ref[0] = high
    low_ref[0] = low


def split_ladder(ladder, counts):
    groups, rows, cols = ladder.shape
    spec = pl.BlockSpec((1, rows, cols), lambda g, c: (g, 0, 0))
    half = jax.ShapeDtypeStruct(ladder.shape, jnp.bfloat16)
    return pl.pallas_call(
        split_kernel,
        grid_spec=pltpu.PrefetchScalarGridSpec(
            num_scalar_prefetch=1, grid=(groups,), in_specs=[spec], out_specs=[spec, spec]
        ),
        out_shape=[half, half],
        compiler_params=pltpu.CompilerParams(vmem_limit_bytes=40 << 20),
        name="split_ladder",
    )(counts, ladder)


def product_kernel(tile_ref, group_ref, bound_ref, rows_ref, high_ref, low_ref, out_ref, rows_high, rows_low):
    visit = pl.program_id(0)
    tile = tile_ref[visit]
    low_row = bound_ref[visit] - tile * TILE
    high_row = bound_ref[visit + 1] - tile * TILE

    @pl.when((visit == 0) | (tile != tile_ref[jnp.maximum(visit - 1, 0)]))
    def _():
        high, low = split(rows_ref[...])
        rows_high[...] = high
        rows_low[...] = low

    @pl.when(high_row > low_row)
    def _():
        def times(a, b):
            return lax.dot_general(a, b, (((1,), (1,)), ((), ())), preferred_element_type=jnp.float32)

        high, low = rows_high[...], rows_low[...]
        weights = high_ref[0]
        product = times(low, weights) + times(high, low_ref[0]) + times(high, weights)
        row = lax.broadcasted_iota(jnp.int32, product.shape, 0)
        out_ref[...] = jnp.where((row >= low_row) & (row < high_row), product, out_ref[...])


def products(rows, high, low, tile, group, bound):
    count, cols = rows.shape
    groups, ab, _ = high.shape
    weights = pl.BlockSpec((1, ab, cols), lambda v, t, g, b: (g[v], 0, 0))
    return pl.pallas_call(
        product_kernel,
        grid_spec=pltpu.PrefetchScalarGridSpec(
            num_scalar_prefetch=3,
            grid=(tile.shape[0],),
            in_specs=[pl.BlockSpec((TILE, cols), lambda v, t, g, b: (t[v], 0)), weights, weights],
            out_specs=pl.BlockSpec((TILE, ab), lambda v, t, g, b: (t[v], 0)),
            scratch_shapes=[pltpu.VMEM((TILE, cols), jnp.bfloat16), pltpu.VMEM((TILE, cols), jnp.bfloat16)],
        ),
        out_shape=jax.ShapeDtypeStruct((count, ab), jnp.float32),
        compiler_params=pltpu.CompilerParams(vmem_limit_bytes=40 << 20),
        name="ladder_products",
    )(tile, group, bound, rows, high, low)


def visits(ends, block_rows, blocks, chunks):
    chunk = jnp.arange(chunks, dtype=jnp.int32)[:, None]
    whole, rest = ends // block_rows, ends % block_rows
    chunk_ends = STEP * whole[None, :] + jnp.clip(rest[None, :] - STEP * chunk, 0, STEP)
    total = STEP * blocks
    tiles = total // TILE
    starts = jnp.broadcast_to(jnp.arange(tiles, dtype=jnp.int32)[None, :] * TILE, (chunks, tiles))
    marks = jnp.concatenate([starts, chunk_ends[:, :-1]], axis=1)
    number = marks.shape[1]
    place = jnp.arange(number, dtype=jnp.int32)
    before = (marks[:, None, :] < marks[:, :, None]) | (
        (marks[:, None, :] == marks[:, :, None]) & (place[None, None, :] < place[None, :, None])
    )
    rank = jnp.sum(before.astype(jnp.int32), axis=2)
    bound = jnp.sum(jnp.where(rank[:, :, None] == place[None, None, :], marks[:, :, None], 0), axis=1)
    tile = jnp.minimum(bound // TILE, tiles - 1)
    group = jnp.sum((chunk_ends[:, None, :] <= bound[:, :, None]).astype(jnp.int32), axis=2)
    group = jnp.minimum(group, ends.shape[0] - 1)
    bound = jnp.concatenate([bound, jnp.full((chunks, 1), total, jnp.int32)], axis=1)
    return tile, group, bound


def body(amplitudes, ladder, pair_energy, vir_energy, occ_count, vir_count):
    groups, ab_local, cd_local = ladder.shape
    plane = lax.axis_size(("col", "ka"))
    device_pos = lax.axis_index(("col", "ka"))
    block_rows = amplitudes.shape[0]
    chunks = block_rows // STEP
    blocks = plane * lax.axis_size("row")
    order = jnp.arange(groups, dtype=jnp.int32)
    ends = jnp.sum(jnp.where(order[None, :] <= order[:, None], occ_count[None, :], 0), axis=1)
    tile, group, bound = visits(ends, block_rows, blocks, chunks)
    high, low = split_ladder(ladder, vir_count - device_pos * cd_local)

    shares = []
    for chunk in range(chunks):
        own = amplitudes[chunk * STEP : (chunk + 1) * STEP].reshape(STEP, plane, cd_local).transpose(1, 0, 2)
        spread = lax.all_to_all(own, ("col", "ka"), split_axis=0, concat_axis=0, tiled=True)
        rows = lax.all_gather(spread, "row", axis=0, tiled=True).reshape(blocks * STEP, cd_local)
        partial = products(rows, high, low, tile[chunk], group[chunk], bound[chunk])
        share = lax.psum_scatter(partial, ("col", "ka"), scatter_dimension=0, tiled=True)
        shares.append(share.reshape(-1, STEP, ab_local))
    share = jnp.stack(shares, axis=1).reshape(-1, ab_local)

    rows_local = share.shape[0]
    row_index = device_pos * rows_local + jnp.arange(rows_local, dtype=jnp.int32)
    row_irrep = jnp.sum((row_index[:, None] >= ends[None, :]).astype(jnp.int32), axis=1)
    onehot = row_irrep[:, None] == order[None, :]
    vir_rows = jnp.sum(jnp.where(onehot[:, :, None], vir_energy[None, :, :], jnp.float32(0.0)), axis=1)
    count_rows = jnp.sum(jnp.where(onehot, vir_count[None, :], 0), axis=1)
    ab_index = lax.axis_index("row") * ab_local + jnp.arange(ab_local, dtype=jnp.int32)
    vir_mask = ab_index[None, :] < count_rows[:, None]
    denom = vir_rows - pair_energy[:, None]
    return jnp.where(vir_mask, share / denom, jnp.float32(0.0))


def solution(mesh):
    placed = (
        P(("row", "col", "ka"), None),
        P(None, "row", ("col", "ka")),
        P(("col", "ka")),
        P(None, "row"),
        P(),
        P(),
    )
    return jax.shard_map(
        body, mesh=mesh, in_specs=placed, out_specs=P(("col", "ka"), "row"), check_vma=False
    )
```

```python
import jax
import jax.numpy as jnp
from jax import lax
from jax.experimental import pallas as pl
from jax.experimental.pallas import tpu as pltpu
from jax.sharding import Mesh, PartitionSpec as P

STEP = 8
TILE = 128
CORES = 2


def split(value):
    high = value.astype(jnp.bfloat16)
    return high, (value - high.astype(jnp.float32)).astype(jnp.bfloat16)


def split_kernel(count_ref, ladder_ref, high_ref, low_ref):
    group = pl.program_id(0)
    value = ladder_ref[0]
    column = lax.broadcasted_iota(jnp.int32, value.shape, 1)
    value = jnp.where(column < count_ref[group], value, jnp.float32(0.0))
    high, low = split(value.T)
    high_ref[0] = high
    low_ref[0] = low


def split_ladder(ladder, counts):
    groups, rows, cols = ladder.shape
    spec = pl.BlockSpec((1, rows, cols), lambda g, c: (g, 0, 0))
    turned = pl.BlockSpec((1, cols, rows), lambda g, c: (g, 0, 0))
    half = jax.ShapeDtypeStruct((groups, cols, rows), jnp.bfloat16)
    return pl.pallas_call(
        split_kernel,
        grid_spec=pltpu.PrefetchScalarGridSpec(
            num_scalar_prefetch=1, grid=(groups,), in_specs=[spec], out_specs=[turned, turned]
        ),
        out_shape=[half, half],
        compiler_params=pltpu.CompilerParams(vmem_limit_bytes=40 << 20),
        cost_estimate=pl.CostEstimate(flops=8 * ladder.size, transcendentals=0, bytes_accessed=8 * ladder.size),
        name="split_ladder",
    )(counts, ladder)


def product_kernel(
    bound_ref, place_ref, own, left, right, far_a, far_b, high, low, mine, other,
    rows, weights_high, weights_low, out, row_sems, weight_sems, out_sems,
):
    groups = high.shape[0]
    plane_rows = own.shape[0]
    planes = rows.shape[0] // plane_rows
    total = rows.shape[0]
    x, core = place_ref[0], place_ref[1]

    def place(step, shift=0):
        return pl.multiple_of(lax.rem(x + step, planes) * plane_rows + shift, STEP)

    half = far_a.shape[0]
    row_copies = [
        pltpu.make_async_copy(source, rows.at[pl.ds(start, source.shape[0])], row_sems.at[i])
        for i, (source, start) in enumerate(
            [
                (own, place(0)),
                (left, place(planes - 1)),
                (right, place(1)),
                (far_a, place(2)),
                (far_b, place(2, half)),
            ]
        )
    ]
    for copy in row_copies:
        copy.start()
    weight_copies = []
    for group in range(groups):
        pair = (
            pltpu.make_async_copy(high.at[group], weights_high.at[group], weight_sems.at[0, group]),
            pltpu.make_async_copy(low.at[group], weights_low.at[group], weight_sems.at[1, group]),
        )
        for copy in pair:
            copy.start()
        weight_copies.append(pair)
    for copy in row_copies:
        copy.wait()

    def times(a, b):
        return lax.dot_general(a, b, (((1,), (0,)), ((), ())), preferred_element_type=jnp.float32)

    for group in range(groups):
        for copy in weight_copies[group]:
            copy.wait()
        first, last = bound_ref[group], bound_ref[group + 1]
        start = lax.div(first, STEP) * STEP
        number = jnp.where(last > first, lax.div(last - start + (TILE - 1), TILE), 0)

        def visit(step, carry, group=group, first=first, last=last, start=start):
            at = pl.multiple_of(jnp.minimum(start + step * TILE, total - TILE), STEP)
            a_high, a_low = split(rows[pl.ds(at, TILE), :])
            weights = weights_high[group]
            product = times(a_low, weights) + times(a_high, weights_low[group]) + times(a_high, weights)
            row = lax.broadcasted_iota(jnp.int32, product.shape, 0) + at
            kept = out[pl.ds(at, TILE), :]
            out[pl.ds(at, TILE), :] = jnp.where((row >= first) & (row < last), product, kept)
            return carry

        lax.fori_loop(0, number, visit, 0)

    pieces, piece_rows, _ = mine.shape
    out_copies = []
    for piece in range(pieces):
        base = piece * CORES * piece_rows
        for kind, (target, which) in enumerate([(other, 1 - core), (mine, core)]):
            start = pl.multiple_of(base + which * piece_rows, STEP)
            copy = pltpu.make_async_copy(
                out.at[pl.ds(start, piece_rows)], target.at[piece], out_sems.at[kind, piece]
            )
            copy.start()
            out_copies.append(copy)
    for copy in out_copies:
        copy.wait()


def products(bound, place, parts, high, low, pieces, piece_rows):
    groups, cols, ab = high.shape
    total = pieces * CORES * piece_rows
    hbm = pl.BlockSpec(memory_space=pltpu.HBM)
    smem = pl.BlockSpec(memory_space=pltpu.SMEM)
    half = jax.ShapeDtypeStruct((pieces, piece_rows, ab), jnp.float32)
    return pl.pallas_call(
        product_kernel,
        in_specs=[smem, smem] + [hbm] * (len(parts) + 2),
        out_specs=[hbm, hbm],
        out_shape=[half, half],
        scratch_shapes=[
            pltpu.VMEM((total, cols), jnp.float32),
            pltpu.VMEM((groups, cols, ab), jnp.bfloat16),
            pltpu.VMEM((groups, cols, ab), jnp.bfloat16),
            pltpu.VMEM((total, ab), jnp.float32),
            pltpu.SemaphoreType.DMA((len(parts),)),
            pltpu.SemaphoreType.DMA((2, groups)),
            pltpu.SemaphoreType.DMA((2, pieces)),
        ],
        compiler_params=pltpu.CompilerParams(vmem_limit_bytes=48 << 20),
        cost_estimate=pl.CostEstimate(
            flops=12 * total * ab * cols, transcendentals=0, bytes_accessed=4 * (groups * ab * cols + total * (ab + cols))
        ),
        name="ladder_products",
    )(bound, place, *parts, high, low)


def ring(size, step):
    return [(i, (i + step) % size) for i in range(size)]


def after(value, *others):
    return lax.optimization_barrier((value, others))[0]


def body(amplitudes, ladder, pair_energy, vir_energy, occ_count, vir_count):
    groups, ab_local, cd_local = ladder.shape
    rows_x, cols_y, depth = lax.axis_size("row"), lax.axis_size("col"), lax.axis_size("deep")
    plane = cols_y * depth * CORES
    x, core = lax.axis_index("row"), lax.axis_index("core")
    device_pos = lax.axis_index(("col", "deep", "core"))
    block_rows = amplitudes.shape[0]
    chunks = block_rows // STEP
    order = jnp.arange(groups, dtype=jnp.int32)
    ends = jnp.sum(jnp.where(order[None, :] <= order[:, None], occ_count[None, :], 0), axis=1)
    within = jnp.arange(chunks, dtype=jnp.int32)[:, None] * STEP
    bounds = STEP * (ends // block_rows)[None, :] + jnp.clip((ends % block_rows)[None, :] - within, 0, STEP)
    bounds = jnp.concatenate([jnp.zeros((chunks, 1), jnp.int32), bounds], axis=1)
    place = jnp.stack([x, core]).astype(jnp.int32)
    high, low = split_ladder(ladder, vir_count - device_pos * cd_local)

    spreads = []
    for chunk in range(chunks):
        rows = amplitudes
        if chunk:
            rows = after(rows, spreads[-1])
        own = rows[chunk * STEP : (chunk + 1) * STEP].reshape(STEP, plane, cd_local).transpose(1, 0, 2)
        spread = lax.all_to_all(own, ("col", "deep", "core"), split_axis=0, concat_axis=0, tiled=True)
        spreads.append(spread.reshape(plane * STEP, cd_local))

    def pair(left, right):
        return lax.ppermute(left, "row", ring(rows_x, 1)), lax.ppermute(right, "row", ring(rows_x, rows_x - 1))

    half = plane * STEP // 2
    near = [pair(spread, spread) for spread in spreads]
    far = [pair(left[:half], right[half:]) for left, right in near]

    parts, shares = [], []
    piece_rows = STEP * rows_x
    for chunk in range(chunks):
        ready = list(near[chunk + 1 : chunk + 2]) + spreads[chunk + 2 : chunk + 3] + parts[-2:-1] + shares[-3:-2]
        inputs = (spreads[chunk], *near[chunk], *far[chunk])
        inputs = after(inputs, *ready)
        mine, other = products(bounds[chunk], place, inputs, high, low, cols_y * depth, piece_rows)
        part = mine + lax.ppermute(other, "core", ring(CORES, 1))
        parts.append(part)
        met = lax.all_to_all(part, ("col", "deep"), split_axis=0, concat_axis=0, tiled=True)
        shares.append(jnp.sum(met, axis=0))
    share = jnp.stack([share.reshape(-1, STEP, ab_local) for share in shares], axis=1).reshape(-1, ab_local)

    rows_local = share.shape[0]
    row_index = device_pos * rows_local + jnp.arange(rows_local, dtype=jnp.int32)
    row_irrep = jnp.sum((row_index[:, None] >= ends[None, :]).astype(jnp.int32), axis=1)
    onehot = row_irrep[:, None] == order[None, :]
    vir_rows = jnp.sum(jnp.where(onehot[:, :, None], vir_energy[None, :, :], jnp.float32(0.0)), axis=1)
    count_rows = jnp.sum(jnp.where(onehot, vir_count[None, :], 0), axis=1)
    ab_index = x * ab_local + jnp.arange(ab_local, dtype=jnp.int32)
    vir_mask = ab_index[None, :] < count_rows[:, None]
    denom = vir_rows - pair_energy[:, None]
    return jnp.where(vir_mask, share / denom, jnp.float32(0.0))


def solution(mesh):
    shape = mesh.devices.shape
    mesh = Mesh(mesh.devices.reshape(shape[0], shape[1], -1, CORES), ("row", "col", "deep", "core"))
    plane = ("col", "deep", "core")
    placed = (
        P(("row", *plane), None),
        P(None, "row", plane),
        P(plane),
        P(None, "row"),
        P(),
        P(),
    )
    return jax.shard_map(
        body, mesh=mesh, in_specs=placed, out_specs=P(plane, "row"), check_vma=False
    )
```

```python
import functools

import jax
import jax.numpy as jnp
from jax import lax
from jax.experimental import pallas as pl
from jax.experimental.pallas import tpu as pltpu
from jax.sharding import Mesh, PartitionSpec as P

STEP = 8
TILE = 128
CORES = 2
UNITS = (1, 1, 1, 1, 1)
AHEAD = 2
EARLY = 2
JOINS = (1, 2, 3, 4, 5)
DIRECT = False
HALVES = True


def split(value):
    high = value.astype(jnp.bfloat16)
    return high, (value - high.astype(jnp.float32)).astype(jnp.bfloat16)


def split_kernel(count_ref, ladder_ref, high_ref, low_ref):
    group = pl.program_id(0)
    value = ladder_ref[0]
    column = lax.broadcasted_iota(jnp.int32, value.shape, 1)
    value = jnp.where(column < count_ref[group], value, jnp.float32(0.0))
    high, low = split(value.T)
    high_ref[0] = high
    low_ref[0] = low


def split_ladder(ladder, counts):
    groups, rows, cols = ladder.shape
    spec = pl.BlockSpec((1, rows, cols), lambda g, c: (g, 0, 0))
    turned = pl.BlockSpec((1, cols, rows), lambda g, c: (g, 0, 0))
    half = jax.ShapeDtypeStruct((groups, cols, rows), jnp.bfloat16)
    return pl.pallas_call(
        split_kernel,
        grid_spec=pltpu.PrefetchScalarGridSpec(
            num_scalar_prefetch=1, grid=(groups,), in_specs=[spec], out_specs=[turned, turned]
        ),
        out_shape=[half, half],
        compiler_params=pltpu.CompilerParams(vmem_limit_bytes=60 << 20),
        cost_estimate=pl.CostEstimate(flops=8 * ladder.size, transcendentals=0, bytes_accessed=4 * ladder.size),
        name="split_ladder",
    )(counts, ladder)


def product_kernel(bound_ref, place_ref, *refs, steps):
    parts = refs[: len(steps)]
    high_ref, low_ref, *targets, rows, out, high, low, row_sems, weight_sems, out_sems = refs[len(steps) :]
    mine, other = targets if len(targets) == 2 else (targets[0], None)
    groups = high.shape[0]
    blocks, sets, step_rows, cols = rows.shape
    unit = sets * step_rows
    tile = TILE // unit
    x, core = place_ref[0], place_ref[1]
    planes = place_ref[2]

    copies = []
    for i, (part, (step, offset, which)) in enumerate(zip(parts, steps)):
        start = lax.rem(x + step, planes) * lax.div(blocks, planes) + offset
        copies.append(
            pltpu.make_async_copy(part, rows.at[pl.ds(start, part.shape[0]), which], row_sems.at[i])
        )
    for copy in copies:
        copy.start()

    def fetch(group):
        return [
            pltpu.make_async_copy(source.at[group], target.at[group], weight_sems.at[i, group])
            for i, (source, target) in enumerate([(high_ref, high), (low_ref, low)])
        ]

    for group in range(AHEAD):
        for copy in fetch(group):
            copy.start()
    for copy in copies:
        copy.wait()

    def times(a, b):
        return lax.dot_general(a, b, (((1,), (0,)), ((), ())), preferred_element_type=jnp.float32)

    for group in range(groups):
        for copy in fetch(group):
            copy.wait()
        if group + AHEAD < groups:
            for copy in fetch(group + AHEAD):
                copy.start()
        first, last = bound_ref[group], bound_ref[group + 1]
        start = lax.div(first, unit)
        number = jnp.where(last > first, lax.div(last - start * unit + (TILE - 1), TILE), 0)

        def visit(turn, carry, group=group, first=first, last=last, start=start):
            at = jnp.minimum(start + turn * tile, blocks - tile)
            a_high, a_low = split(rows[pl.ds(at, tile)].reshape(TILE, cols))
            weights = high[group]
            product = times(a_low, weights) + times(a_high, low[group]) + times(a_high, weights)
            row = lax.broadcasted_iota(jnp.int32, product.shape, 0) + at * unit
            kept = out[pl.ds(at, tile)].reshape(product.shape)
            product = jnp.where((row >= first) & (row < last), product, kept)
            out[pl.ds(at, tile)] = product.reshape(tile, sets, step_rows, product.shape[1])
            return carry

        lax.fori_loop(0, number, visit, 0)

    if other is None:
        copy = pltpu.make_async_copy(out, mine, out_sems.at[0, 0])
        copy.start()
        copy.wait()
        return
    pieces, piece_blocks = mine.shape[:2]
    copies = []
    for piece in range(pieces):
        for kind, (target, which) in enumerate([(other, 1 - core), (mine, core)]):
            start = (piece * CORES + which) * piece_blocks
            copy = pltpu.make_async_copy(
                out.at[pl.ds(start, piece_blocks)], target.at[piece], out_sems.at[kind, piece]
            )
            copy.start()
            copies.append(copy)
    for copy in copies:
        copy.wait()


def products(bound, place, parts, steps, high, low, pieces, blocks, sets, whole):
    groups, cols, ab = high.shape
    hbm = pl.BlockSpec(memory_space=pltpu.HBM)
    smem = pl.BlockSpec(memory_space=pltpu.SMEM)
    shapes = [jax.ShapeDtypeStruct((pieces, blocks // pieces // CORES, sets, STEP, ab), jnp.float32)] * 2
    if whole:
        shapes = [jax.ShapeDtypeStruct((blocks, sets, STEP, ab), jnp.float32)]
    total = blocks * sets * STEP
    return pl.pallas_call(
        functools.partial(product_kernel, steps=steps),
        in_specs=[smem, smem] + [hbm] * (len(parts) + 2),
        out_specs=[hbm] * len(shapes),
        out_shape=shapes,
        scratch_shapes=[
            pltpu.VMEM((blocks, sets, STEP, cols), jnp.float32),
            pltpu.VMEM((blocks, sets, STEP, ab), jnp.float32),
            pltpu.VMEM((groups, cols, ab), jnp.bfloat16),
            pltpu.VMEM((groups, cols, ab), jnp.bfloat16),
            pltpu.SemaphoreType.DMA((len(parts),)),
            pltpu.SemaphoreType.DMA((2, groups)),
            pltpu.SemaphoreType.DMA((2, pieces)),
        ],
        compiler_params=pltpu.CompilerParams(vmem_limit_bytes=60 << 20),
        cost_estimate=pl.CostEstimate(
            flops=12 * total * ab * cols, transcendentals=0, bytes_accessed=4 * total * (ab + cols)
        ),
        name="ladder_products",
    )(bound, place, *parts, high, low)


def ring(size, step):
    return [(i, (i + step) % size) for i in range(size)]


def after(value, *others):
    return lax.optimization_barrier((value, others))[0]


def body(amplitudes, ladder, pair_energy, vir_energy, occ_count, vir_count):
    groups, ab_local, cd_local = ladder.shape
    rows_x, cols_y, depth = lax.axis_size("row"), lax.axis_size("col"), lax.axis_size("deep")
    plane = cols_y * depth * CORES
    x, core = lax.axis_index("row"), lax.axis_index("core")
    device_pos = lax.axis_index(("col", "deep", "core"))
    block_rows = amplitudes.shape[0]
    chunks = block_rows // STEP
    order = jnp.arange(groups, dtype=jnp.int32)
    ends = jnp.sum(jnp.where(order[None, :] <= order[:, None], occ_count[None, :], 0), axis=1)
    place = jnp.stack([x, core, rows_x]).astype(jnp.int32)
    high, low = split_ladder(ladder, vir_count - device_pos * cd_local)

    spreads = []
    for chunk in range(chunks):
        rows = amplitudes
        if chunk:
            rows = after(rows, spreads[-1], *([high] if chunk == EARLY else []))
        own = rows[chunk * STEP : (chunk + 1) * STEP].reshape(STEP, plane, cd_local).transpose(1, 0, 2)
        spread = lax.all_to_all(own, ("col", "deep", "core"), split_axis=0, concat_axis=0, tiled=True)
        spreads.append(spread)

    def pair(left, right):
        return lax.ppermute(left, "row", ring(rows_x, 1)), lax.ppermute(right, "row", ring(rows_x, rows_x - 1))

    near = [pair(spread, spread) for spread in spreads]
    half = plane // 2
    far_last = pair(near[-1][0][:half], near[-1][1][half:])
    parts, shares = [], []
    chunk = 0
    for sets in UNITS:
        inputs, steps = [], []
        for which in range(sets):
            left, right = near[chunk + which]
            inputs += [spreads[chunk + which], left, right]
            steps += [(0, 0, which), (rows_x - 1, 0, which), (1, 0, which)]
        if sets == 1:
            if chunk + 1 == chunks or HALVES:
                last = chunk + 1 == chunks
                inputs += far_last if last else pair(near[chunk][0][:half], near[chunk][1][half:])
                steps += [(2, 0, 0), (2, half, 0)]
            else:
                turn = rows_x - 1 if chunk % 2 else 1
                inputs.append(lax.ppermute(near[chunk][chunk % 2], "row", ring(rows_x, turn)))
                steps.append((2, 0, 0))
        else:
            inputs += pair(near[chunk][0], near[chunk + 1][1])
            steps += [(2, 0, 0), (2, 0, 1)]
        begin = STEP * chunk
        unit = STEP * sets
        bound = unit * (ends // block_rows) + jnp.clip(ends % block_rows - begin, 0, unit)
        bound = jnp.concatenate([jnp.zeros((1,), jnp.int32), bound])
        chunk += sets
        ready = near[chunk : chunk + 1] + spreads[chunk + 1 : chunk + 2] + parts[-2:-1]
        if len(shares) > 1:
            ready += shares[len(parts) - 3 : len(parts) - 2]
        number = len(parts)
        whole = DIRECT and chunk == chunks
        made = products(
            bound, place, after(tuple(inputs), *ready), tuple(steps), high, low,
            cols_y * depth, plane * rows_x, sets, whole,
        )
        if whole:
            part = made[0].reshape(plane, rows_x, sets, STEP, ab_local)
            met = lax.all_to_all(part, ("col", "deep", "core"), split_axis=0, concat_axis=0, tiled=True)
            shares.append(jnp.sum(met, axis=0))
            break
        other = made[1]
        if chunk + 1 == chunks:
            other = after(other, *far_last)
        parts.append(made[0] + lax.ppermute(other, "core", ring(CORES, 1)))
        if number + 1 in JOINS:
            group = parts[len(shares) :]
            if len(group) == 1:
                met = lax.all_to_all(group[0], ("col", "deep"), split_axis=0, concat_axis=0, tiled=True)
                shares.append(jnp.sum(met, axis=0))
            else:
                met = lax.all_to_all(
                    jnp.stack(group, axis=1), ("col", "deep"), split_axis=0, concat_axis=0, tiled=True
                )
                met = jnp.sum(met, axis=0)
                shares += [met[i] for i in range(len(group))]
    share = jnp.concatenate(shares, axis=1).reshape(-1, ab_local)

    rows_local = share.shape[0]
    row_index = device_pos * rows_local + jnp.arange(rows_local, dtype=jnp.int32)
    row_irrep = jnp.sum((row_index[:, None] >= ends[None, :]).astype(jnp.int32), axis=1)
    onehot = row_irrep[:, None] == order[None, :]
    vir_rows = jnp.sum(jnp.where(onehot[:, :, None], vir_energy[None, :, :], jnp.float32(0.0)), axis=1)
    count_rows = jnp.sum(jnp.where(onehot, vir_count[None, :], 0), axis=1)
    ab_index = x * ab_local + jnp.arange(ab_local, dtype=jnp.int32)
    vir_mask = ab_index[None, :] < count_rows[:, None]
    denom = vir_rows - pair_energy[:, None]
    return jnp.where(vir_mask, share / denom, jnp.float32(0.0))


def solution(mesh):
    shape = mesh.devices.shape
    mesh = Mesh(mesh.devices.reshape(shape[0], shape[1], -1, CORES), ("row", "col", "deep", "core"))
    plane = ("col", "deep", "core")
    placed = (
        P(("row", *plane), None),
        P(None, "row", plane),
        P(plane),
        P(None, "row"),
        P(),
        P(),
    )
    return jax.shard_map(
        body, mesh=mesh, in_specs=placed, out_specs=P(plane, "row"), check_vma=False
    )
```

```python
import functools

import jax
import jax.numpy as jnp
from jax import lax
from jax.experimental import pallas as pl
from jax.experimental.pallas import tpu as pltpu
from jax.sharding import Mesh, PartitionSpec as P

STEP = 8
TILE = 128
CORES = 2
UNITS = (1, 1, 1, 1, 1)
AHEAD = 3
EARLY = 2
JOINS = (1, 2, 3, 4, 5)
DIRECT = False
HALVES = True


def split(value):
    high = value.astype(jnp.bfloat16)
    return high, (value - high.astype(jnp.float32)).astype(jnp.bfloat16)


def split_kernel(count_ref, ladder_ref, high_ref, low_ref):
    group = pl.program_id(0)
    value = ladder_ref[0]
    column = lax.broadcasted_iota(jnp.int32, value.shape, 1)
    value = jnp.where(column < count_ref[group], value, jnp.float32(0.0))
    high, low = split(value.T)
    high_ref[0] = high
    low_ref[0] = low


def split_ladder(ladder, counts):
    groups, rows, cols = ladder.shape
    spec = pl.BlockSpec((1, rows, cols), lambda g, c: (g, 0, 0))
    turned = pl.BlockSpec((1, cols, rows), lambda g, c: (g, 0, 0))
    half = jax.ShapeDtypeStruct((groups, cols, rows), jnp.bfloat16)
    return pl.pallas_call(
        split_kernel,
        grid_spec=pltpu.PrefetchScalarGridSpec(
            num_scalar_prefetch=1, grid=(groups,), in_specs=[spec], out_specs=[turned, turned]
        ),
        out_shape=[half, half],
        compiler_params=pltpu.CompilerParams(vmem_limit_bytes=60 << 20),
        cost_estimate=pl.CostEstimate(flops=8 * ladder.size, transcendentals=0, bytes_accessed=4 * ladder.size),
        name="split_ladder",
    )(counts, ladder)


def product_kernel(bound_ref, place_ref, *refs, steps):
    parts = refs[: len(steps)]
    high_ref, low_ref, *targets, rows, out, high, low, row_sems, weight_sems, out_sems = refs[len(steps) :]
    mine, other = targets if len(targets) == 2 else (targets[0], None)
    groups = high.shape[0]
    blocks, sets, step_rows, cols = rows.shape
    unit = sets * step_rows
    tile = TILE // unit
    x, core = place_ref[0], place_ref[1]
    planes = place_ref[2]

    copies = []
    for i, (part, (step, offset, which)) in enumerate(zip(parts, steps)):
        start = lax.rem(x + step, planes) * lax.div(blocks, planes) + offset
        copies.append(
            pltpu.make_async_copy(part, rows.at[pl.ds(start, part.shape[0]), which], row_sems.at[i])
        )
    for copy in copies:
        copy.start()

    def fetch(group):
        return [
            pltpu.make_async_copy(source.at[group], target.at[group], weight_sems.at[i, group])
            for i, (source, target) in enumerate([(high_ref, high), (low_ref, low)])
        ]

    for group in range(AHEAD):
        for copy in fetch(group):
            copy.start()
    for copy in copies:
        copy.wait()

    def times(a, b):
        return lax.dot_general(a, b, (((1,), (0,)), ((), ())), preferred_element_type=jnp.float32)

    for group in range(groups):
        for copy in fetch(group):
            copy.wait()
        if group + AHEAD < groups:
            for copy in fetch(group + AHEAD):
                copy.start()
        first, last = bound_ref[group], bound_ref[group + 1]
        start = lax.div(first, unit)
        number = jnp.where(last > first, lax.div(last - start * unit + (TILE - 1), TILE), 0)

        def visit(turn, carry, group=group, first=first, last=last, start=start):
            at = jnp.minimum(start + turn * tile, blocks - tile)
            a_high, a_low = split(rows[pl.ds(at, tile)].reshape(TILE, cols))
            weights = high[group]
            product = times(a_low, weights) + times(a_high, low[group]) + times(a_high, weights)
            row = lax.broadcasted_iota(jnp.int32, product.shape, 0) + at * unit
            kept = out[pl.ds(at, tile)].reshape(product.shape)
            product = jnp.where((row >= first) & (row < last), product, kept)
            out[pl.ds(at, tile)] = product.reshape(tile, sets, step_rows, product.shape[1])
            return carry

        lax.fori_loop(0, number, visit, 0)

    if other is None:
        copy = pltpu.make_async_copy(out, mine, out_sems.at[0, 0])
        copy.start()
        copy.wait()
        return
    pieces, piece_blocks = mine.shape[:2]
    copies = []
    for piece in range(pieces):
        for kind, (target, which) in enumerate([(other, 1 - core), (mine, core)]):
            start = (piece * CORES + which) * piece_blocks
            copy = pltpu.make_async_copy(
                out.at[pl.ds(start, piece_blocks)], target.at[piece], out_sems.at[kind, piece]
            )
            copy.start()
            copies.append(copy)
    for copy in copies:
        copy.wait()


def products(bound, place, parts, steps, high, low, pieces, blocks, sets, whole):
    groups, cols, ab = high.shape
    hbm = pl.BlockSpec(memory_space=pltpu.HBM)
    smem = pl.BlockSpec(memory_space=pltpu.SMEM)
    shapes = [jax.ShapeDtypeStruct((pieces, blocks // pieces // CORES, sets, STEP, ab), jnp.float32)] * 2
    if whole:
        shapes = [jax.ShapeDtypeStruct((blocks, sets, STEP, ab), jnp.float32)]
    total = blocks * sets * STEP
    return pl.pallas_call(
        functools.partial(product_kernel, steps=steps),
        in_specs=[smem, smem] + [hbm] * (len(parts) + 2),
        out_specs=[hbm] * len(shapes),
        out_shape=shapes,
        scratch_shapes=[
            pltpu.VMEM((blocks, sets, STEP, cols), jnp.float32),
            pltpu.VMEM((blocks, sets, STEP, ab), jnp.float32),
            pltpu.VMEM((groups, cols, ab), jnp.bfloat16),
            pltpu.VMEM((groups, cols, ab), jnp.bfloat16),
            pltpu.SemaphoreType.DMA((len(parts),)),
            pltpu.SemaphoreType.DMA((2, groups)),
            pltpu.SemaphoreType.DMA((2, pieces)),
        ],
        compiler_params=pltpu.CompilerParams(vmem_limit_bytes=60 << 20),
        cost_estimate=pl.CostEstimate(
            flops=12 * total * ab * cols, transcendentals=0, bytes_accessed=4 * total * (ab + cols)
        ),
        name="ladder_products",
    )(bound, place, *parts, high, low)


def ring(size, step):
    return [(i, (i + step) % size) for i in range(size)]


def after(value, *others):
    return lax.optimization_barrier((value, others))[0]


def body(amplitudes, ladder, pair_energy, vir_energy, occ_count, vir_count):
    groups, ab_local, cd_local = ladder.shape
    rows_x, cols_y, depth = lax.axis_size("row"), lax.axis_size("col"), lax.axis_size("deep")
    plane = cols_y * depth * CORES
    x, core = lax.axis_index("row"), lax.axis_index("core")
    device_pos = lax.axis_index(("col", "deep", "core"))
    block_rows = amplitudes.shape[0]
    chunks = block_rows // STEP
    order = jnp.arange(groups, dtype=jnp.int32)
    ends = jnp.sum(jnp.where(order[None, :] <= order[:, None], occ_count[None, :], 0), axis=1)
    place = jnp.stack([x, core, rows_x]).astype(jnp.int32)
    high, low = split_ladder(ladder, vir_count - device_pos * cd_local)

    spreads = []
    for chunk in range(chunks):
        rows = amplitudes
        if chunk:
            rows = after(rows, spreads[-1], *([high] if chunk == EARLY else []))
        own = rows[chunk * STEP : (chunk + 1) * STEP].reshape(STEP, plane, cd_local).transpose(1, 0, 2)
        spread = lax.all_to_all(own, ("col", "deep", "core"), split_axis=0, concat_axis=0, tiled=True)
        spreads.append(spread)

    def pair(left, right):
        return lax.ppermute(left, "row", ring(rows_x, 1)), lax.ppermute(right, "row", ring(rows_x, rows_x - 1))

    near = [pair(spread, spread) for spread in spreads]
    half = plane // 2
    far_last = pair(near[-1][0][:half], near[-1][1][half:])
    parts, shares = [], []
    chunk = 0
    for sets in UNITS:
        inputs, steps = [], []
        for which in range(sets):
            left, right = near[chunk + which]
            inputs += [spreads[chunk + which], left, right]
            steps += [(0, 0, which), (rows_x - 1, 0, which), (1, 0, which)]
        if sets == 1:
            if chunk + 1 == chunks or HALVES:
                last = chunk + 1 == chunks
                inputs += far_last if last else pair(near[chunk][0][:half], near[chunk][1][half:])
                steps += [(2, 0, 0), (2, half, 0)]
            else:
                turn = rows_x - 1 if chunk % 2 else 1
                inputs.append(lax.ppermute(near[chunk][chunk % 2], "row", ring(rows_x, turn)))
                steps.append((2, 0, 0))
        else:
            inputs += pair(near[chunk][0], near[chunk + 1][1])
            steps += [(2, 0, 0), (2, 0, 1)]
        begin = STEP * chunk
        unit = STEP * sets
        bound = unit * (ends // block_rows) + jnp.clip(ends % block_rows - begin, 0, unit)
        bound = jnp.concatenate([jnp.zeros((1,), jnp.int32), bound])
        chunk += sets
        ready = near[chunk : chunk + 1] + spreads[chunk + 1 : chunk + 2] + parts[-2:-1]
        if len(shares) > 1:
            ready += shares[len(parts) - 3 : len(parts) - 2]
        number = len(parts)
        whole = DIRECT and chunk == chunks
        made = products(
            bound, place, after(tuple(inputs), *ready), tuple(steps), high, low,
            cols_y * depth, plane * rows_x, sets, whole,
        )
        if whole:
            part = made[0].reshape(plane, rows_x, sets, STEP, ab_local)
            met = lax.all_to_all(part, ("col", "deep", "core"), split_axis=0, concat_axis=0, tiled=True)
            shares.append(jnp.sum(met, axis=0))
            break
        other = made[1]
        if chunk + 1 == chunks:
            other = after(other, *far_last)
        parts.append(made[0] + lax.ppermute(other, "core", ring(CORES, 1)))
        if number + 1 in JOINS:
            group = parts[len(shares) :]
            if len(group) == 1:
                met = lax.all_to_all(group[0], ("col", "deep"), split_axis=0, concat_axis=0, tiled=True)
                shares.append(jnp.sum(met, axis=0))
            else:
                met = lax.all_to_all(
                    jnp.stack(group, axis=1), ("col", "deep"), split_axis=0, concat_axis=0, tiled=True
                )
                met = jnp.sum(met, axis=0)
                shares += [met[i] for i in range(len(group))]
    share = jnp.concatenate(shares, axis=1).reshape(-1, ab_local)

    rows_local = share.shape[0]
    row_index = device_pos * rows_local + jnp.arange(rows_local, dtype=jnp.int32)
    row_irrep = jnp.sum((row_index[:, None] >= ends[None, :]).astype(jnp.int32), axis=1)
    onehot = row_irrep[:, None] == order[None, :]
    vir_rows = jnp.sum(jnp.where(onehot[:, :, None], vir_energy[None, :, :], jnp.float32(0.0)), axis=1)
    count_rows = jnp.sum(jnp.where(onehot, vir_count[None, :], 0), axis=1)
    ab_index = x * ab_local + jnp.arange(ab_local, dtype=jnp.int32)
    vir_mask = ab_index[None, :] < count_rows[:, None]
    denom = vir_rows - pair_energy[:, None]
    return jnp.where(vir_mask, share / denom, jnp.float32(0.0))


def solution(mesh):
    shape = mesh.devices.shape
    mesh = Mesh(mesh.devices.reshape(shape[0], shape[1], -1, CORES), ("row", "col", "deep", "core"))
    plane = ("col", "deep", "core")
    placed = (
        P(("row", *plane), None),
        P(None, "row", plane),
        P(plane),
        P(None, "row"),
        P(),
        P(),
    )
    return jax.shard_map(
        body, mesh=mesh, in_specs=placed, out_specs=P(plane, "row"), check_vma=False
    )
```
